256 devices in a mesh: rows: 16 (over y, x), feat: 16 (over z, core).
Axes of the slice: x: 4, y: 4, z: 8, core: 2. Of those that a mesh axis runs over, the one named last changes fastest.
Arguments:
- feature_bins: int32 [512, 131072], P('feat', 'rows'), may hold values from 0 to 127
- leaf_index: int32 [131072], P('rows'), may hold values from 0 to 63
- doc_scores: float32 [131072], P('rows'), may hold values from -8 to 256
- doc_weights: float32 [131072], P('rows'), may hold values from 0.3 to 3
- destination: int32 [131072], P('rows'), may hold values from 0 to 131071, as said below
- query_ids: int32 [131072], P('rows'), may hold values from 0 to 131071, as said below
- clicks: int32 [131072], P('rows'), may hold values 0 or 1
Outputs:
- histograms: float32 [64, 512, 2, 128], P('rows', 'feat')
The draws below stay inside these ranges and needn't reach their ends.
Inputs may be any that keep to these rules, and one draw needn't show every extreme that they name: A permutation of the slots; document i goes to owner destination // 8192, slot destination % 8192; each device's 8192 documents hold exactly 512 for every owner. `query_ids`: a query's id is the number of its last slot; each query's slots are consecutive, lie in one aligned block of 256 slots and hold 1 to 256 slots; every owner's slots hold a query of exactly 256.
All inputs are finite; a program needn't handle non-finite values. No bound on the sum of `clicks` on one device may be relied on, other than what follows from the above.
Results may differ from the reference program's by a relative error of at most 0.0023.
Values may be sent and summed in bfloat16 or wider, within the bound.
No kernel may reach another device: no remote copies, remote signals or barrier semaphores. Data moves between devices by JAX's collectives and lax.ppermute only.
A program may use at most 64 MiB of HBM per device.

```python
import math
import jax
import jax.numpy as jnp
from jax import lax

F = 512
BINS = 128
LEAVES = 64
QBLOCK = 256
DOC_DEV = 8192
DOCS = 131072
N_ROWS = 16


def routing(key):
    folded = jax.random.fold_in(key, 101)
    first, second = jax.random.split(folded, 2)
    shuffles = jax.vmap(lambda subkey: jax.random.permutation(subkey, DOC_DEV))(jax.random.split(first, N_ROWS))
    capacity = DOC_DEV // N_ROWS
    owner_base = jnp.arange(N_ROWS, dtype=jnp.int32)[:, None, None] * DOC_DEV
    owner_blocks = shuffles.reshape(N_ROWS, N_ROWS, capacity).astype(jnp.int32) + owner_base
    per_source = jnp.transpose(owner_blocks, (1, 0, 2)).reshape(N_ROWS, DOC_DEV)
    mixed = jax.vmap(lambda subkey, entries: jax.random.permutation(subkey, entries))(jax.random.split(second, N_ROWS), per_source)
    return mixed.reshape(DOCS).astype(jnp.int32)


def draw_destination(key, part):
    return routing(key)


def draw_query_ids(key, part):
    folded = jax.random.fold_in(key, 202)
    first, second = jax.random.split(folded, 2)
    position = jnp.arange(DOCS, dtype=jnp.int32)
    block_end = position % QBLOCK == QBLOCK - 1
    cuts = jax.random.randint(first, (DOCS,), 0, 64) == 0
    chosen = jax.random.randint(second, (N_ROWS,), 0, DOC_DEV // QBLOCK)
    block_index = position // QBLOCK % (DOC_DEV // QBLOCK)
    whole = block_index == chosen[position // DOC_DEV]
    ends = jnp.where(whole, block_end, block_end | cuts)
    marked = jnp.where(ends, position, DOCS - 1).astype(jnp.int32)
    return lax.cummin(marked, axis=0, reverse=True).astype(jnp.int32)


def draw_doc_scores(key, part):
    placed = routing(key)
    folded = jax.random.fold_in(key, 303)
    first = jax.random.fold_in(folded, 0)
    noise = jnp.clip(jax.random.normal(first, (DOCS,), jnp.float32), -4.0, 4.0)
    owner_values = 2.0 * noise
    return owner_values[placed].astype(jnp.float32)


def place_ends(array, rng, least, top_value):
    place = [jax.random.randint(jax.random.fold_in(rng, axis), (), 0, length) for axis, length in enumerate(array.shape)]
    longest = array.shape.index(max(array.shape))
    next_to = place[:longest] + [(place[longest] + 1) % array.shape[longest]] + place[longest + 1:]
    return array.at[tuple(place)].set(least).at[tuple(next_to)].set(top_value)


def block_scale(own_key, extent, cuts, least, largest):
    level, own = 1.0, jax.random.fold_in(own_key, 6)
    for dim, parts in cuts:
        draws = jnp.exp(jax.random.uniform(jax.random.fold_in(own, dim), (parts,), jnp.float32, least / len(cuts), largest / len(cuts)))
        level = level * jnp.repeat(draws, extent[dim] // parts).reshape([-1 if axis == dim else 1 for axis in range(len(extent))])
    return level


def setup_inputs(seed: int = 0) -> dict:
    seeds = jax.random.split(jax.random.key(seed), 8)
    return {
        "feature_bins": place_ends(jax.random.randint(seeds[0], (F, DOCS), 0, BINS), jax.random.fold_in(seeds[0], 1), 0, BINS - 1).astype(jnp.int32),
        "leaf_index": place_ends(jax.random.randint(seeds[1], (DOCS,), 0, LEAVES), jax.random.fold_in(seeds[1], 1), 0, LEAVES - 1).astype(jnp.int32),
        "doc_scores": draw_doc_scores(jax.random.fold_in(seeds[7], 71), 0),
        "doc_weights": jnp.clip(jnp.exp(math.log(3.0) - 2.3025851 * jax.random.uniform(seeds[3], (DOCS,), jnp.float32) ** block_scale(seeds[3], (DOCS,), ((0, 16),), -0.2, 0.2)), 0.3, 3.0),
        "destination": draw_destination(jax.random.fold_in(seeds[7], 71), 0),
        "query_ids": draw_query_ids(jax.random.fold_in(seeds[7], 71), 0),
        "clicks": place_ends((jax.random.randint(seeds[6], (DOCS,), 0, 3) < 1).astype(jnp.int32), jax.random.fold_in(seeds[6], 1), 0, 1),
    }


def reference(feature_bins, leaf_index, doc_scores, doc_weights, destination, query_ids, clicks):
    owner_scores = jnp.zeros((DOCS,), jnp.float32).at[destination].set(doc_scores)
    owner_weights = jnp.zeros((DOCS,), jnp.float32).at[destination].set(doc_weights)
    targets = clicks.astype(jnp.float32)
    query_top = jax.ops.segment_max(owner_scores, query_ids, num_segments=DOCS)
    scaled = owner_weights * jnp.exp(owner_scores - query_top[query_ids])
    denominator = jax.ops.segment_sum(scaled, query_ids, num_segments=DOCS)[query_ids]
    clicked = jax.ops.segment_sum(owner_weights * targets, query_ids, num_segments=DOCS)[query_ids]
    chance = scaled / denominator
    gradient = (owner_weights * targets - clicked * chance).astype(jnp.bfloat16)
    curvature = (clicked * chance * (1.0 - chance)).astype(jnp.bfloat16)
    doc_stats = jnp.stack([gradient, curvature], axis=1)[destination].astype(jnp.float32)

    def per_feature(column):
        bucket = leaf_index * BINS + column
        return jax.ops.segment_sum(doc_stats, bucket, num_segments=LEAVES * BINS)

    columns_hist = lax.map(per_feature, feature_bins)
    histograms = columns_hist.reshape(F, LEAVES, BINS, 2)
    return jnp.transpose(histograms, (1, 0, 3, 2))
```

```python
import jax
import jax.numpy as jnp
from jax import lax
from jax.experimental import pallas as pl
from jax.experimental.pallas import tpu as pltpu
from jax.sharding import PartitionSpec as P

BINS = 128
LEAVES = 64
QBLOCK = 256
OWNERS = 16
DOC = 8192
F_DEV = 32
CH = 1024
F32 = jnp.float32
BF16 = jnp.bfloat16
I32 = jnp.int32


def nt(a, b):
    return lax.dot_general(a, b, (((1,), (1,)), ((), ())), preferred_element_type=F32)


def nn(a, b):
    return lax.dot_general(a, b, (((1,), (0,)), ((), ())), preferred_element_type=F32)


def lanes(tile):
    return jnp.concatenate([tile[r : r + 1, :] for r in range(tile.shape[0])], axis=1)


def rows16(row):
    return jnp.broadcast_to(row.astype(F32), (16, row.shape[1])).astype(BF16)


def iota_bf16(shape, fn):
    parts = [lax.broadcasted_iota(I32, shape, d) for d in range(len(shape))]
    return fn(*parts).astype(F32).astype(BF16)


def split3(x):
    a = x.astype(BF16).astype(F32)
    r = x - a
    b = r.astype(BF16).astype(F32)
    return a, b, r - b


def one_hot(row, width, cols):
    it = iota_bf16((width // 16, 16, cols), lambda g, s, c: g * 16 + s)
    hit = it == rows16(row)[None]
    one = jnp.ones((), BF16)
    zero = jnp.zeros((), BF16)
    return jnp.where(hit, one, zero).reshape(width, cols)


def route_body(dest_ref, score_ref, weight_ref, send_ref, pos_ref, a_ref, b_ref):
    dest = dest_ref[...]
    owner = dest >> 13
    masks = jnp.concatenate(
        [jnp.where(owner == o, 1.0, 0.0).astype(F32) for o in range(OWNERS)], axis=0
    ).astype(BF16)
    r = lax.broadcasted_iota(I32, (128, 256), 0)
    c = lax.broadcasted_iota(I32, (128, 256), 1)
    tri = jnp.where((r < c) | (c >= 128), 1.0, 0.0).astype(F32).astype(BF16)
    counts = nn(masks, tri)
    prefix = counts[:, :128]
    totals = counts[:, 128:].astype(BF16)
    wide = jnp.concatenate([totals[o * 64 : (o + 1) * 64] for o in range(OWNERS)], axis=1)
    r = lax.broadcasted_iota(I32, (64, 64), 0)
    c = lax.broadcasted_iota(I32, (64, 64), 1)
    low = jnp.where(c < r, 1.0, 0.0).astype(F32).astype(BF16)
    before = nn(low, wide)
    rank = jnp.zeros((64, 128), F32)
    for o in range(OWNERS):
        here = prefix[o * 64 : (o + 1) * 64] + before[:, o * 128 : (o + 1) * 128]
        rank = jnp.where(owner == o, here, rank)
    pos_ref[...] = owner * 512 + rank.astype(I32)

    sub = lax.broadcasted_iota(I32, (8, CH), 0)
    target = iota_bf16((8, 16, CH), lambda g, s, c: (g * 2 + s // 8) * 2 + s % 2)

    def chunk(t, carry):
        rows = pl.ds(pl.multiple_of(t * 8, 8), 8)
        cols = pl.ds(pl.multiple_of(t * CH, CH), CH)
        pos = lanes(pos_ref[rows, :])
        slot = lanes(dest_ref[rows, :]) & (DOC - 1)
        s3 = split3(lanes(score_ref[rows, :]))
        w3 = split3(lanes(weight_ref[rows, :]))
        d3 = ((slot & 8128).astype(F32), (slot & 63).astype(F32), jnp.zeros((1, CH), F32))
        b_ref[:, cols] = one_hot(pos & 255, 256, CH)
        hit = target == rows16(pos >> 8)[None]
        for p in range(3):
            full = lambda v: jnp.broadcast_to(v, (8, CH))
            vals = jnp.where(sub < 2, full(s3[p]), jnp.where(sub < 4, full(w3[p]), full(d3[p])))
            both = jnp.concatenate([vals, vals], axis=0).astype(BF16)
            a_ref[p * 128 : (p + 1) * 128, cols] = jnp.where(
                hit, both[None], jnp.zeros((), BF16)
            ).reshape(128, CH)
        return carry

    lax.fori_loop(0, DOC // CH, chunk, 0)
    table = nt(a_ref[...], b_ref[...])
    send_ref[...] = (table[0:128] + table[128:256] + table[256:384]).reshape(OWNERS, 8, 256)


def route(dest, score, weight):
    return pl.pallas_call(
        route_body,
        out_shape=(
            jax.ShapeDtypeStruct((OWNERS, 8, 256), F32),
            jax.ShapeDtypeStruct((64, 128), I32),
        ),
        scratch_shapes=[pltpu.VMEM((384, DOC), BF16), pltpu.VMEM((256, DOC), BF16)],
        name="route",
    )(dest, score, weight)


def owner_body(rec_ref, query_ref, clicks_ref, out_ref, a_ref, b_ref, h_ref):
    def chunk(o, carry):
        tile = rec_ref[o]
        cols = pl.ds(pl.multiple_of(o * 512, 512), 512)
        pick = lambda n: jnp.concatenate([tile[2 * n : 2 * n + 1], tile[2 * n + 1 : 2 * n + 2]], axis=1)
        slot = pick(2).astype(I32)
        b_ref[:, cols] = one_hot(slot & 255, 256, 512)
        block = slot >> 8
        h_ref[pl.ds(o, 1), :] = block
        it = iota_bf16((2, 16, 512), lambda g, s, c: g * 16 + s)
        hit = it == rows16(block)[None]
        for n in range(2):
            for p, v in enumerate(split3(pick(n))):
                at = (p * 2 + n) * 32
                a_ref[at : at + 32, cols] = jnp.where(
                    hit, rows16(v)[None], jnp.zeros((), BF16)
                ).reshape(32, 512)
        return carry

    lax.fori_loop(0, OWNERS, chunk, 0)
    table = nt(a_ref[...], b_ref[...])
    table = table[0:64] + table[64:128] + table[128:192]
    score = table[0:32]
    weight = table[32:64]

    def wide(ref):
        return jnp.concatenate([ref[pl.ds(0, 32, stride=2), :], ref[pl.ds(1, 32, stride=2), :]], axis=1)

    query = wide(query_ref)
    clicks = wide(clicks_ref)
    lane = lax.broadcasted_iota(I32, (32, 256), 1)
    first = lane
    same = []
    for k in range(8):
        d = 1 << k
        same.append((pltpu.roll(query, d, 1) == query) & (lane >= d))

    def scan(x, op):
        for k in range(8):
            d = 1 << k
            x = jnp.where(same[k], op(x, pltpu.roll(x, d, 1)), x)
        return x

    back = []
    for k in range(8):
        d = 1 << k
        back.append((pltpu.roll(query, 256 - d, 1) == query) & (lane < 256 - d))

    def spread(x, op):
        for k in range(8):
            d = 1 << k
            x = jnp.where(back[k], op(x, pltpu.roll(x, 256 - d, 1)), x)
        return x

    last = (query & 255) == lane
    top = spread(scan(score, jnp.maximum), jnp.maximum)
    scaled = weight * jnp.exp(score - top)
    gain = weight * clicks.astype(F32)
    total = lambda x: spread(jnp.where(last, scan(x, jnp.add), 0.0), jnp.add)
    denominator = total(scaled)
    clicked = total(gain)
    chance = scaled / denominator
    gradient = (gain - clicked * chance).astype(BF16)
    curvature = (clicked * chance * (1.0 - chance)).astype(BF16)
    stats = jnp.concatenate([gradient, curvature], axis=0)
    picked = nn(stats, b_ref[...])
    sub = lax.broadcasted_iota(I32, (32, 128), 0)
    for o in range(OWNERS):
        rows = []
        for q in range(4):
            at = o * 512 + q * 128
            hit = sub == h_ref[o : o + 1, q * 128 : (q + 1) * 128]
            for k in range(2):
                part = picked[k * 32 : (k + 1) * 32, at : at + 128]
                rows.append(jnp.sum(jnp.where(hit, part, 0.0), axis=0, keepdims=True))
        out_ref[o] = jnp.concatenate(rows, axis=0)


def owner(rec, query, clicks):
    return pl.pallas_call(
        owner_body,
        out_shape=jax.ShapeDtypeStruct((OWNERS, 8, 128), F32),
        scratch_shapes=[
            pltpu.VMEM((192, DOC), BF16),
            pltpu.VMEM((256, DOC), BF16),
            pltpu.VMEM((OWNERS, 512), I32),
        ],
        name="owner",
    )(rec, query, clicks)


def hist_body(back_ref, pos_ref, leaf_ref, bins_ref, send_ref, spread_ref):
    table = back_ref[...].reshape(128, 128).astype(BF16)

    def expand(t, carry):
        rows = pl.ds(pl.multiple_of(t * 8, 8), 8)
        pos = lanes(pos_ref[rows, :])
        leaf = lanes(leaf_ref[rows, :])
        picked = nn(table, one_hot(pos & 127, 128, CH))
        hi = jnp.broadcast_to(pos >> 7, (8, CH))
        quarter = lax.broadcasted_iota(I32, (8, CH), 0) // 2
        acc = jnp.zeros((8, CH), F32)
        for o in range(OWNERS):
            acc = acc + jnp.where(hi == quarter + 4 * o, picked[o * 8 : (o + 1) * 8], 0.0)
        acc = acc + pltpu.roll(acc, 4, 0)
        acc = acc + pltpu.roll(acc, 2, 0)
        both = jnp.concatenate([acc, acc], axis=0).astype(BF16)
        it = iota_bf16((8, 16, CH), lambda g, s, c: g * 8 + s // 2)
        spread_ref[:, pl.ds(pl.multiple_of(t * CH, CH), CH)] = jnp.where(
            it == rows16(leaf)[None], both[None], jnp.zeros((), BF16)
        ).reshape(128, CH)
        return carry

    lax.fori_loop(0, DOC // CH, expand, 0)

    def pair(p, carry):
        def part(t, acc):
            cols = pl.ds(pl.multiple_of(t * CH, CH), CH)
            hot = jnp.concatenate(
                [one_hot(bins_ref[pl.ds(2 * p + j, 1), cols], 128, CH) for j in range(2)], axis=0
            )
            return acc + nt(spread_ref[:, cols], hot)

        acc = lax.fori_loop(0, DOC // CH, part, jnp.zeros((128, 256), F32))
        left = acc[:, :128].reshape(OWNERS, 1, 8, 128)
        right = acc[:, 128:].reshape(OWNERS, 1, 8, 128)
        send_ref[:, pl.ds(p, 1)] = (
            jnp.concatenate([left, right], axis=1).reshape(OWNERS, 1, 16, 128).astype(BF16)
        )
        return carry

    lax.fori_loop(0, F_DEV // 2, pair, 0)


def hist(back, pos, leaf, bins):
    return pl.pallas_call(
        hist_body,
        out_shape=jax.ShapeDtypeStruct((OWNERS, F_DEV // 2, 16, 128), BF16),
        scratch_shapes=[pltpu.VMEM((128, DOC), BF16)],
        name="hist",
    )(back, pos, leaf, bins)


def total_body(rec_ref, out_ref):
    for p in range(F_DEV // 2):
        acc = rec_ref[0, p].astype(F32)
        for o in range(1, OWNERS):
            acc = acc + rec_ref[o, p].astype(F32)
        for j in range(2):
            for l in range(4):
                out_ref[l, 4 * p + 2 * j : 4 * p + 2 * j + 2, :] = acc[8 * j + 2 * l : 8 * j + 2 * l + 2]


def total(rec):
    return pl.pallas_call(
        total_body, out_shape=jax.ShapeDtypeStruct((4, 2 * F_DEV, 128), F32), name="total"
    )(rec)


def shards(feature_bins, leaf_index, doc_scores, doc_weights, destination, query_ids, clicks):
    tall = lambda a: a.reshape(64, 128)
    swap = lambda a: lax.all_to_all(a, "rows", split_axis=0, concat_axis=0, tiled=True)
    send, pos = route(tall(destination), tall(doc_scores), tall(doc_weights))
    back = owner(swap(send), tall(query_ids), tall(clicks))
    parts = hist(swap(back), pos, tall(leaf_index), feature_bins)
    return total(swap(parts)).reshape(4, F_DEV, 2, BINS)


def solution(mesh):
    placed = (P("feat", "rows"), P("rows"), P("rows"), P("rows"), P("rows"), P("rows"), P("rows"))
    return jax.shard_map(
        shards, mesh=mesh, in_specs=placed, out_specs=P("rows", "feat", None, None), check_vma=False
    )
```

```python
import jax
import jax.numpy as jnp
from jax import lax
from jax.experimental import pallas as pl
from jax.experimental.pallas import tpu as pltpu
from jax.sharding import PartitionSpec as P

BINS = 128
LEAVES = 64
QBLOCK = 256
OWNERS = 16
DOC = 8192
F_DEV = 32
CH = 1024
F32 = jnp.float32
BF16 = jnp.bfloat16
I32 = jnp.int32


def nt(a, b):
    return lax.dot_general(a, b, (((1,), (1,)), ((), ())), preferred_element_type=F32)


def nn(a, b):
    return lax.dot_general(a, b, (((1,), (0,)), ((), ())), preferred_element_type=F32)


def lanes(tile):
    return jnp.concatenate([tile[r : r + 1, :] for r in range(tile.shape[0])], axis=1)


def rows16(row):
    return jnp.broadcast_to(row.astype(F32), (16, row.shape[1])).astype(BF16)


def iota_bf16(shape, fn):
    parts = [lax.broadcasted_iota(I32, shape, d) for d in range(len(shape))]
    return fn(*parts).astype(F32).astype(BF16)


def split3(x):
    a = x.astype(BF16).astype(F32)
    r = x - a
    b = r.astype(BF16).astype(F32)
    return a, b, r - b


def one_hot(row, width, cols):
    it = iota_bf16((width // 16, 16, cols), lambda g, s, c: g * 16 + s)
    hit = it == rows16(row)[None]
    one = jnp.ones((), BF16)
    zero = jnp.zeros((), BF16)
    return jnp.where(hit, one, zero).reshape(width, cols)


def route_body(dest_ref, score_ref, weight_ref, send_ref, pos_ref, a_ref, b_ref):
    dest = dest_ref[...]
    owner = dest >> 13
    masks = jnp.concatenate(
        [jnp.where(owner == o, 1.0, 0.0).astype(F32) for o in range(OWNERS)], axis=0
    ).astype(BF16)
    r = lax.broadcasted_iota(I32, (128, 256), 0)
    c = lax.broadcasted_iota(I32, (128, 256), 1)
    tri = jnp.where((r < c) | (c >= 128), 1.0, 0.0).astype(F32).astype(BF16)
    counts = nn(masks, tri)
    prefix = counts[:, :128]
    totals = counts[:, 128:].astype(BF16)
    wide = jnp.concatenate([totals[o * 64 : (o + 1) * 64] for o in range(OWNERS)], axis=1)
    r = lax.broadcasted_iota(I32, (64, 64), 0)
    c = lax.broadcasted_iota(I32, (64, 64), 1)
    low = jnp.where(c < r, 1.0, 0.0).astype(F32).astype(BF16)
    before = nn(low, wide)
    rank = jnp.zeros((64, 128), F32)
    for o in range(OWNERS):
        here = prefix[o * 64 : (o + 1) * 64] + before[:, o * 128 : (o + 1) * 128]
        rank = jnp.where(owner == o, here, rank)
    pos_ref[...] = owner * 512 + rank.astype(I32)

    sub = lax.broadcasted_iota(I32, (8, CH), 0)
    target = iota_bf16((8, 16, CH), lambda g, s, c: (g * 2 + s // 8) * 2 + s % 2)

    def chunk(t, carry):
        rows = pl.ds(pl.multiple_of(t * 8, 8), 8)
        cols = pl.ds(pl.multiple_of(t * CH, CH), CH)
        pos = lanes(pos_ref[rows, :])
        slot = lanes(dest_ref[rows, :]) & (DOC - 1)
        s3 = split3(lanes(score_ref[rows, :]))
        w3 = split3(lanes(weight_ref[rows, :]))
        d3 = ((slot & 8128).astype(F32), (slot & 63).astype(F32), jnp.zeros((1, CH), F32))
        b_ref[:, cols] = one_hot(pos & 255, 256, CH)
        hit = target == rows16(pos >> 8)[None]
        for p in range(3):
            full = lambda v: jnp.broadcast_to(v, (8, CH))
            vals = jnp.where(sub < 2, full(s3[p]), jnp.where(sub < 4, full(w3[p]), full(d3[p])))
            both = jnp.concatenate([vals, vals], axis=0).astype(BF16)
            a_ref[p * 128 : (p + 1) * 128, cols] = jnp.where(
                hit, both[None], jnp.zeros((), BF16)
            ).reshape(128, CH)
        return carry

    lax.fori_loop(0, DOC // CH, chunk, 0)
    table = nt(a_ref[...], b_ref[...])
    send_ref[...] = (table[0:128] + table[128:256] + table[256:384]).reshape(OWNERS, 8, 256)


def route(dest, score, weight):
    return pl.pallas_call(
        route_body,
        out_shape=(
            jax.ShapeDtypeStruct((OWNERS, 8, 256), F32),
            jax.ShapeDtypeStruct((64, 128), I32),
        ),
        scratch_shapes=[pltpu.VMEM((384, DOC), BF16), pltpu.VMEM((256, DOC), BF16)],
        name="route",
    )(dest, score, weight)


def owner_body(rec_ref, query_ref, clicks_ref, out_ref, a_ref, b_ref, h_ref):
    def chunk(o, carry):
        tile = rec_ref[o]
        cols = pl.ds(pl.multiple_of(o * 512, 512), 512)
        pick = lambda n: jnp.concatenate([tile[2 * n : 2 * n + 1], tile[2 * n + 1 : 2 * n + 2]], axis=1)
        slot = pick(2).astype(I32)
        b_ref[:, cols] = one_hot(slot & 255, 256, 512)
        block = slot >> 8
        h_ref[pl.ds(o, 1), :] = block
        it = iota_bf16((2, 16, 512), lambda g, s, c: g * 16 + s)
        hit = it == rows16(block)[None]
        for n in range(2):
            for p, v in enumerate(split3(pick(n))):
                at = (p * 2 + n) * 32
                a_ref[at : at + 32, cols] = jnp.where(
                    hit, rows16(v)[None], jnp.zeros((), BF16)
                ).reshape(32, 512)
        return carry

    lax.fori_loop(0, OWNERS, chunk, 0)
    table = nt(a_ref[...], b_ref[...])
    table = table[0:64] + table[64:128] + table[128:192]
    score = table[0:32]
    weight = table[32:64]

    def wide(ref):
        return jnp.concatenate([ref[pl.ds(0, 32, stride=2), :], ref[pl.ds(1, 32, stride=2), :]], axis=1)

    query = wide(query_ref)
    clicks = wide(clicks_ref)
    lane = lax.broadcasted_iota(I32, (32, 256), 1)
    first = lane
    same = []
    for k in range(8):
        d = 1 << k
        same.append((pltpu.roll(query, d, 1) == query) & (lane >= d))

    def scan(x, op):
        for k in range(8):
            d = 1 << k
            x = jnp.where(same[k], op(x, pltpu.roll(x, d, 1)), x)
        return x

    back = []
    for k in range(8):
        d = 1 << k
        back.append((pltpu.roll(query, 256 - d, 1) == query) & (lane < 256 - d))

    def spread(x, op):
        for k in range(8):
            d = 1 << k
            x = jnp.where(back[k], op(x, pltpu.roll(x, 256 - d, 1)), x)
        return x

    last = (query & 255) == lane
    top = spread(scan(score, jnp.maximum), jnp.maximum)
    scaled = weight * jnp.exp(score - top)
    gain = weight * clicks.astype(F32)
    total = lambda x: spread(jnp.where(last, scan(x, jnp.add), 0.0), jnp.add)
    denominator = total(scaled)
    clicked = total(gain)
    chance = scaled / denominator
    gradient = (gain - clicked * chance).astype(BF16)
    curvature = (clicked * chance * (1.0 - chance)).astype(BF16)
    stats = jnp.concatenate([gradient, curvature], axis=0)
    picked = nn(stats, b_ref[...])
    sub = lax.broadcasted_iota(I32, (32, 128), 0)
    for o in range(OWNERS):
        rows = []
        for q in range(4):
            at = o * 512 + q * 128
            hit = sub == h_ref[o : o + 1, q * 128 : (q + 1) * 128]
            for k in range(2):
                part = picked[k * 32 : (k + 1) * 32, at : at + 128]
                rows.append(jnp.sum(jnp.where(hit, part, 0.0), axis=0, keepdims=True))
        out_ref[o] = jnp.concatenate(rows, axis=0)


def owner(rec, query, clicks):
    return pl.pallas_call(
        owner_body,
        out_shape=jax.ShapeDtypeStruct((OWNERS, 8, 128), F32),
        scratch_shapes=[
            pltpu.VMEM((192, DOC), BF16),
            pltpu.VMEM((256, DOC), BF16),
            pltpu.VMEM((OWNERS, 512), I32),
        ],
        name="owner",
    )(rec, query, clicks)


F8 = jnp.float8_e4m3fn
LOW = 16.0
GF = 4


def one_hot8(row, cols):
    it = (lax.broadcasted_iota(I32, (4, 32, cols), 0) * 32 + lax.broadcasted_iota(I32, (4, 32, cols), 1)).astype(jnp.int8)
    r = jnp.broadcast_to(row, (32, cols)).astype(jnp.int8)
    return jnp.where(it == r[None], jnp.ones((), F8), jnp.zeros((), F8)).reshape(128, cols)


def hist_body(back_ref, pos_ref, leaf_ref, bins_ref, send_ref, spread_ref):
    back = back_ref[...].reshape(128, 128)
    table = back.astype(BF16)
    sub8 = lax.broadcasted_iota(I32, (8, 128), 0)
    peak = jnp.max(jnp.abs(back_ref[...]), axis=0)
    peak = jnp.max(peak, axis=1, keepdims=True)
    odd = lax.broadcasted_iota(I32, (8, 1), 0) % 2
    top0 = jnp.max(jnp.where(odd == 0, peak, 0.0), axis=0, keepdims=True)
    top1 = jnp.max(jnp.where(odd == 1, peak, 0.0), axis=0, keepdims=True)
    top = jnp.where(odd == 0, top0, top1)
    up = jnp.full((8, 1), 2.0**-20, F32)
    down = jnp.full((8, 1), 2.0**20, F32)
    for e in (64, 32, 16, 8, 4, 2, 1):
        fits = top * (up * 2.0**e) <= 448.0
        up = jnp.where(fits, up * 2.0**e, up)
        down = jnp.where(fits, down * 2.0**-e, down)
    up = jnp.broadcast_to(up, (8, CH))

    def expand(t, carry):
        rows = pl.ds(pl.multiple_of(t * 8, 8), 8)
        pos = lanes(pos_ref[rows, :])
        leaf = lanes(leaf_ref[rows, :])
        picked = nn(table, one_hot(pos & 127, 128, CH))
        hi = jnp.broadcast_to(pos >> 7, (8, CH))
        quarter = lax.broadcasted_iota(I32, (8, CH), 0) // 2
        acc = jnp.zeros((8, CH), F32)
        for o in range(OWNERS):
            acc = acc + jnp.where(hi == quarter + 4 * o, picked[o * 8 : (o + 1) * 8], 0.0)
        acc = acc + pltpu.roll(acc, 4, 0)
        acc = acc + pltpu.roll(acc, 2, 0)
        acc = acc * up
        high = acc.astype(F8).astype(F32)
        low = (acc - high) * LOW
        it = iota_bf16((8, 16, CH), lambda g, s, c: g * 8 + s // 2)
        hit = it == rows16(leaf)[None]
        for n, v in enumerate((high, low)):
            both = jnp.concatenate([v, v], axis=0).astype(BF16)
            spread_ref[n * 128 : (n + 1) * 128, pl.ds(pl.multiple_of(t * CH, CH), CH)] = (
                jnp.where(hit, both[None], jnp.zeros((), BF16)).reshape(128, CH).astype(F8)
            )
        return carry

    lax.fori_loop(0, DOC // CH, expand, 0)
    scale = jnp.broadcast_to(down, (8, 128))[None]

    def group(p, carry):
        hot = jnp.concatenate([one_hot8(bins_ref[pl.ds(GF * p + j, 1), :], DOC) for j in range(GF)], axis=0)
        acc = nt(spread_ref[...], hot)
        acc = acc[:128] + acc[128:] * (1.0 / LOW)
        cut = [(acc[:, 128 * j : 128 * j + 128].reshape(OWNERS, 8, 128) * scale).reshape(OWNERS, 1, 8, 128) for j in range(GF)]
        send_ref[:, pl.ds(p * (GF // 2), GF // 2)] = (
            jnp.concatenate(cut, axis=1).reshape(OWNERS, GF // 2, 16, 128).astype(BF16)
        )
        return carry

    lax.fori_loop(0, F_DEV // GF, group, 0)


def hist(back, pos, leaf, bins):
    return pl.pallas_call(
        hist_body,
        out_shape=jax.ShapeDtypeStruct((OWNERS, F_DEV // 2, 16, 128), BF16),
        scratch_shapes=[pltpu.VMEM((256, DOC), F8)],
        name="hist",
    )(back, pos, leaf, bins)


def total_body(rec_ref, out_ref):
    for p in range(F_DEV // 2):
        acc = rec_ref[0, p].astype(F32)
        for o in range(1, OWNERS):
            acc = acc + rec_ref[o, p].astype(F32)
        for j in range(2):
            for l in range(4):
                out_ref[l, 4 * p + 2 * j : 4 * p + 2 * j + 2, :] = acc[8 * j + 2 * l : 8 * j + 2 * l + 2]


def total(rec):
    return pl.pallas_call(
        total_body, out_shape=jax.ShapeDtypeStruct((4, 2 * F_DEV, 128), F32), name="total"
    )(rec)


def shards(feature_bins, leaf_index, doc_scores, doc_weights, destination, query_ids, clicks):
    tall = lambda a: a.reshape(64, 128)
    swap = lambda a: lax.all_to_all(a, "rows", split_axis=0, concat_axis=0, tiled=True)
    send, pos = route(tall(destination), tall(doc_scores), tall(doc_weights))
    back = owner(swap(send), tall(query_ids), tall(clicks))
    parts = hist(swap(back), pos, tall(leaf_index), feature_bins)
    return total(swap(parts)).reshape(4, F_DEV, 2, BINS)


def solution(mesh):
    placed = (P("feat", "rows"), P("rows"), P("rows"), P("rows"), P("rows"), P("rows"), P("rows"))
    return jax.shard_map(
        shards, mesh=mesh, in_specs=placed, out_specs=P("rows", "feat", None, None), check_vma=False
    )
```

```python
import jax
import jax.numpy as jnp
from jax import lax
from jax.experimental import pallas as pl
from jax.experimental.pallas import tpu as pltpu
from jax.sharding import PartitionSpec as P

BINS = 128
LEAVES = 64
QBLOCK = 256
OWNERS = 16
DOC = 8192
F_DEV = 32
CH = 1024
F32 = jnp.float32
BF16 = jnp.bfloat16
I32 = jnp.int32


def nt(a, b):
    return lax.dot_general(a, b, (((1,), (1,)), ((), ())), preferred_element_type=F32)


def nn(a, b):
    return lax.dot_general(a, b, (((1,), (0,)), ((), ())), preferred_element_type=F32)


def lanes(tile):
    return jnp.concatenate([tile[r : r + 1, :] for r in range(tile.shape[0])], axis=1)


def rows16(row):
    return jnp.broadcast_to(row.astype(F32), (16, row.shape[1])).astype(BF16)


def iota_bf16(shape, fn):
    parts = [lax.broadcasted_iota(I32, shape, d) for d in range(len(shape))]
    return fn(*parts).astype(F32).astype(BF16)


def split3(x):
    a = x.astype(BF16).astype(F32)
    r = x - a
    b = r.astype(BF16).astype(F32)
    return a, b, r - b


def one_hot(row, width, cols):
    it = iota_bf16((width // 16, 16, cols), lambda g, s, c: g * 16 + s)
    hit = it == rows16(row)[None]
    one = jnp.ones((), BF16)
    zero = jnp.zeros((), BF16)
    return jnp.where(hit, one, zero).reshape(width, cols)


def route_body(dest_ref, score_ref, weight_ref, send_ref, pos_ref, a_ref, b_ref):
    dest = dest_ref[...]
    owner = dest >> 13
    masks = jnp.concatenate(
        [jnp.where(owner == o, 1.0, 0.0).astype(F32) for o in range(OWNERS)], axis=0
    ).astype(BF16)
    r = lax.broadcasted_iota(I32, (128, 256), 0)
    c = lax.broadcasted_iota(I32, (128, 256), 1)
    tri = jnp.where((r < c) | (c >= 128), 1.0, 0.0).astype(F32).astype(BF16)
    counts = nn(masks, tri)
    prefix = counts[:, :128]
    totals = counts[:, 128:].astype(BF16)
    wide = jnp.concatenate([totals[o * 64 : (o + 1) * 64] for o in range(OWNERS)], axis=1)
    r = lax.broadcasted_iota(I32, (64, 64), 0)
    c = lax.broadcasted_iota(I32, (64, 64), 1)
    low = jnp.where(c < r, 1.0, 0.0).astype(F32).astype(BF16)
    before = nn(low, wide)
    rank = jnp.zeros((64, 128), F32)
    for o in range(OWNERS):
        here = prefix[o * 64 : (o + 1) * 64] + before[:, o * 128 : (o + 1) * 128]
        rank = jnp.where(owner == o, here, rank)

    sub = lax.broadcasted_iota(I32, (8, CH), 0)
    target = iota_bf16((8, 16, CH), lambda g, s, c: (g * 2 + s // 8) * 2 + s % 2)

    score = split3(score_ref[...])
    weight = split3(weight_ref[...])
    slot = dest & (DOC - 1)
    zero = jnp.zeros((64, 128), F32)
    fields = (
        (score[0], weight[0], (slot & 8128).astype(F32), score[2]),
        (score[1], weight[1], (slot & 63).astype(F32), zero),
    )
    place = owner * 512 + rank.astype(I32)
    pos_ref[...] = place
    for t in range(DOC // CH):
        rows = slice(t * 8, t * 8 + 8)
        cols = slice(t * CH, t * CH + CH)
        pos = lanes(place[rows])
        b_ref[:, cols] = one_hot(pos & 255, 256, CH)
        hit = target == rows16(pos >> 8)[None]
        for p in range(2):
            part = [jnp.broadcast_to(lanes(v[rows]), (8, CH)) for v in fields[p]]
            vals = jnp.where(
                sub < 4,
                jnp.where(sub < 2, part[0], part[1]),
                jnp.where(sub < 6, part[2], part[3]),
            )
            both = jnp.concatenate([vals, vals], axis=0).astype(BF16)
            a_ref[p * 128 : (p + 1) * 128, cols] = jnp.where(
                hit, both[None], jnp.zeros((), BF16)
            ).reshape(128, CH)
    table = nt(a_ref[...], b_ref[...])
    send_ref[...] = (table[0:128] + table[128:256]).reshape(OWNERS, 8, 256)


def route(dest, score, weight):
    return pl.pallas_call(
        route_body,
        out_shape=(
            jax.ShapeDtypeStruct((OWNERS, 8, 256), F32),
            jax.ShapeDtypeStruct((64, 128), I32),
        ),
        scratch_shapes=[pltpu.VMEM((256, DOC), BF16), pltpu.VMEM((256, DOC), BF16)],
        in_specs=[pl.BlockSpec(memory_space=pltpu.VMEM)] * 3,
        out_specs=(pl.BlockSpec(memory_space=pltpu.VMEM), pl.BlockSpec(memory_space=pltpu.VMEM)),
        compiler_params=pltpu.CompilerParams(vmem_limit_bytes=24 << 20),
        name="route",
    )(dest, score, weight)


def owner_body(rec_ref, query_ref, clicks_ref, out_ref, a_ref, b_ref, h_ref):
    it = iota_bf16((2, 16, 512), lambda g, s, c: g * 16 + s)
    for o in range(OWNERS):
        tile = rec_ref[o]
        cols = slice(o * 512, o * 512 + 512)
        pick = lambda n: jnp.concatenate([tile[2 * n : 2 * n + 1], tile[2 * n + 1 : 2 * n + 2]], axis=1)
        slot = pick(2).astype(I32)
        b_ref[:, cols] = one_hot(slot & 255, 256, 512)
        block = slot >> 8
        h_ref[o : o + 1, :] = block
        hit = it == rows16(block)[None]
        s3 = split3(pick(0) + pick(3))
        w3 = split3(pick(1))
        for n, v in enumerate((s3[0], w3[0], s3[1], w3[1], s3[2])):
            a_ref[n * 32 : n * 32 + 32, cols] = jnp.where(
                hit, rows16(v)[None], jnp.zeros((), BF16)
            ).reshape(32, 512)
    table = nt(a_ref[...], b_ref[...])
    score = table[0:32] + table[64:96] + table[128:160]
    weight = table[32:64] + table[96:128]

    def wide(ref):
        return jnp.concatenate([ref[pl.ds(0, 32, stride=2), :], ref[pl.ds(1, 32, stride=2), :]], axis=1)

    query = wide(query_ref)
    clicks = wide(clicks_ref)
    lane = lax.broadcasted_iota(I32, (32, 256), 1)
    steps = [1 << k for k in range(8)]
    fore = [(pltpu.roll(query, d, 1) == query) & (lane >= d) for d in steps]
    back = [(pltpu.roll(query, 256 - d, 1) == query) & (lane < 256 - d) for d in steps]

    def scans(x, op):
        y = x
        for d, f, b in zip(steps, fore, back):
            x = jnp.where(f, op(x, pltpu.roll(x, d, 1)), x)
            y = jnp.where(b, op(y, pltpu.roll(y, 256 - d, 1)), y)
        return x, y

    top = jnp.maximum(*scans(score, jnp.maximum))
    scaled = weight * jnp.exp(score - top)
    gain = weight * clicks.astype(F32)

    def total(x):
        left, right = scans(x, jnp.add)
        return left + (right - x)

    denominator = total(scaled)
    clicked = total(gain)
    chance = scaled / denominator
    gradient = (gain - clicked * chance).astype(BF16)
    curvature = (clicked * chance * (1.0 - chance)).astype(BF16)
    stats = jnp.concatenate([gradient, curvature], axis=0)
    picked = nn(stats, b_ref[...])
    sub = lax.broadcasted_iota(I32, (32, 128), 0)
    for o in range(OWNERS):
        rows = []
        for q in range(4):
            at = o * 512 + q * 128
            hit = sub == h_ref[o : o + 1, q * 128 : (q + 1) * 128]
            for k in range(2):
                part = picked[k * 32 : (k + 1) * 32, at : at + 128]
                rows.append(jnp.sum(jnp.where(hit, part, 0.0), axis=0, keepdims=True))
        out_ref[o] = jnp.concatenate(rows, axis=0)


def owner(rec, query, clicks):
    return pl.pallas_call(
        owner_body,
        out_shape=jax.ShapeDtypeStruct((OWNERS, 8, 128), F32),
        scratch_shapes=[
            pltpu.VMEM((160, DOC), BF16),
            pltpu.VMEM((256, DOC), BF16),
            pltpu.VMEM((OWNERS, 512), I32),
        ],
        in_specs=[pl.BlockSpec(memory_space=pltpu.VMEM)] * 3,
        out_specs=pl.BlockSpec(memory_space=pltpu.VMEM),
        compiler_params=pltpu.CompilerParams(vmem_limit_bytes=24 << 20),
        name="owner",
    )(rec, query, clicks)


F8 = jnp.float8_e4m3fn
LOW = 16.0
GF = 8
PB = 8


def one_hot8(row, cols):
    it = (lax.broadcasted_iota(I32, (4, 32, cols), 0) * 32 + lax.broadcasted_iota(I32, (4, 32, cols), 1)).astype(jnp.int8)
    r = jnp.broadcast_to(row, (32, cols)).astype(jnp.int8)
    return jnp.where(it == r[None], jnp.ones((), F8), jnp.zeros((), F8)).reshape(128, cols)


def hist_body(back_ref, pos_ref, leaf_ref, bins_ref, send_ref, spread_ref, down_ref):
    @pl.when(pl.program_id(0) == 0)
    def _():
        back = back_ref[...].reshape(128, 128)
        table = back.astype(BF16)
        sub8 = lax.broadcasted_iota(I32, (8, 128), 0)
        peak = jnp.max(jnp.abs(back_ref[...]), axis=0)
        peak = jnp.max(peak, axis=1, keepdims=True)
        odd = lax.broadcasted_iota(I32, (8, 1), 0) % 2
        top0 = jnp.max(jnp.where(odd == 0, peak, 0.0), axis=0, keepdims=True)
        top1 = jnp.max(jnp.where(odd == 1, peak, 0.0), axis=0, keepdims=True)
        top = jnp.where(odd == 0, top0, top1)
        up = jnp.full((8, 1), 2.0**-20, F32)
        down = jnp.full((8, 1), 2.0**20, F32)
        for e in (64, 32, 16, 8, 4, 2, 1):
            fits = top * (up * 2.0**e) <= 448.0
            up = jnp.where(fits, up * 2.0**e, up)
            down = jnp.where(fits, down * 2.0**-e, down)
        up = jnp.broadcast_to(up, (8, CH))

        for t in range(DOC // CH):
            rows = slice(t * 8, t * 8 + 8)
            pos = lanes(pos_ref[rows, :])
            leaf = lanes(leaf_ref[rows, :])
            picked = nn(table, one_hot(pos & 127, 128, CH))
            hi = jnp.broadcast_to(pos >> 7, (8, CH))
            quarter = lax.broadcasted_iota(I32, (8, CH), 0) // 2
            acc = jnp.zeros((8, CH), F32)
            for o in range(OWNERS):
                acc = acc + jnp.where(hi == quarter + 4 * o, picked[o * 8 : (o + 1) * 8], 0.0)
            acc = acc + pltpu.roll(acc, 4, 0)
            acc = acc + pltpu.roll(acc, 2, 0)
            acc = acc * up
            high = acc.astype(F8).astype(F32)
            low = (acc - high) * LOW
            it = iota_bf16((8, 16, CH), lambda g, s, c: g * 8 + s // 2)
            hit = it == rows16(leaf)[None]
            for n, v in enumerate((high, low)):
                both = jnp.concatenate([v, v], axis=0).astype(BF16)
                spread_ref[n * 128 : (n + 1) * 128, t * CH : t * CH + CH] = (
                    jnp.where(hit, both[None], jnp.zeros((), BF16)).reshape(128, CH).astype(F8)
                )
        down_ref[...] = jnp.broadcast_to(down, (8, 128))

    scale = down_ref[...][None]
    hot = jnp.concatenate([one_hot8(bins_ref[j : j + 1, :], DOC) for j in range(GF)], axis=0)
    acc = nt(spread_ref[...], hot)
    acc = acc[:128] + acc[128:] * (1.0 / LOW)
    cut = [
        (acc[:, 128 * j : 128 * j + 128].reshape(OWNERS, 8, 128) * scale).reshape(OWNERS, 1, 8, 128)
        for j in range(GF)
    ]
    send_ref[...] = (
        jnp.concatenate(cut, axis=1).reshape(OWNERS, GF // 2, 16, 128).astype(BF16)
    )


def hist(back, pos, leaf, bins):
    whole = lambda a: pl.BlockSpec(a.shape, lambda p: (0,) * a.ndim)
    return pl.pallas_call(
        hist_body,
        grid=(F_DEV // GF,),
        in_specs=[whole(back), whole(pos), whole(leaf), pl.BlockSpec((GF, DOC), lambda p: (p, 0))],
        out_specs=pl.BlockSpec((OWNERS, GF // 2, 16, 128), lambda p: (0, p, 0, 0)),
        out_shape=jax.ShapeDtypeStruct((OWNERS, F_DEV // 2, 16, 128), BF16),
        scratch_shapes=[pltpu.VMEM((256, DOC), F8), pltpu.VMEM((8, 128), F32)],
        compiler_params=pltpu.CompilerParams(vmem_limit_bytes=40 << 20),
        name="hist",
    )(back, pos, leaf, bins)


def total_body(rec_ref, out_ref):
    for p in range(PB):
        acc = rec_ref[0, p].astype(F32)
        for o in range(1, OWNERS):
            acc = acc + rec_ref[o, p].astype(F32)
        for j in range(2):
            for l in range(4):
                out_ref[l, 4 * p + 2 * j : 4 * p + 2 * j + 2, :] = acc[8 * j + 2 * l : 8 * j + 2 * l + 2]


def total(rec):
    return pl.pallas_call(
        total_body,
        grid=(F_DEV // 2 // PB,),
        in_specs=[pl.BlockSpec((OWNERS, PB, 16, 128), lambda p: (0, p, 0, 0))],
        out_specs=pl.BlockSpec((4, 4 * PB, 128), lambda p: (0, p, 0)),
        out_shape=jax.ShapeDtypeStruct((4, 2 * F_DEV, 128), F32),
        compiler_params=pltpu.CompilerParams(vmem_limit_bytes=16 << 20),
        name="total",
    )(rec)


def shards(feature_bins, leaf_index, doc_scores, doc_weights, destination, query_ids, clicks):
    tall = lambda a: a.reshape(64, 128)
    swap = lambda a: lax.all_to_all(a, "rows", split_axis=0, concat_axis=0, tiled=True)
    send, pos = route(tall(destination), tall(doc_scores), tall(doc_weights))
    back = owner(swap(send), tall(query_ids), tall(clicks))
    parts = hist(swap(back), pos, tall(leaf_index), feature_bins)
    return total(swap(parts)).reshape(4, F_DEV, 2, BINS)


def solution(mesh):
    placed = (P("feat", "rows"), P("rows"), P("rows"), P("rows"), P("rows"), P("rows"), P("rows"))
    return jax.shard_map(
        shards, mesh=mesh, in_specs=placed, out_specs=P("rows", "feat", None, None), check_vma=False
    )
```

```python
import jax
import jax.numpy as jnp
from jax import lax
from jax.experimental import pallas as pl
from jax.experimental.pallas import tpu as pltpu
from jax.sharding import PartitionSpec as P

BINS = 128
LEAVES = 64
QBLOCK = 256
OWNERS = 16
DOC = 8192
F_DEV = 32
CH = 1024
F32 = jnp.float32
BF16 = jnp.bfloat16
I32 = jnp.int32


def nt(a, b):
    return lax.dot_general(a, b, (((1,), (1,)), ((), ())), preferred_element_type=F32)


def nn(a, b):
    return lax.dot_general(a, b, (((1,), (0,)), ((), ())), preferred_element_type=F32)


def lanes(tile):
    return jnp.concatenate([tile[r : r + 1, :] for r in range(tile.shape[0])], axis=1)


def rows16(row):
    return jnp.broadcast_to(row.astype(F32), (16, row.shape[1])).astype(BF16)


def iota_bf16(shape, fn):
    parts = [lax.broadcasted_iota(I32, shape, d) for d in range(len(shape))]
    return fn(*parts).astype(F32).astype(BF16)


def split3(x):
    a = x.astype(BF16).astype(F32)
    r = x - a
    b = r.astype(BF16).astype(F32)
    return a, b, r - b


def one_hot(row, width, cols):
    it = iota_bf16((width // 16, 16, cols), lambda g, s, c: g * 16 + s)
    hit = it == rows16(row)[None]
    one = jnp.ones((), BF16)
    zero = jnp.zeros((), BF16)
    return jnp.where(hit, one, zero).reshape(width, cols)


def route_body(docs_ref, send_ref, pos_ref, a_ref, b_ref):
    dest = docs_ref[0].astype(I32)
    owner = dest >> 13
    masks = jnp.concatenate(
        [jnp.where(owner == o, 1.0, 0.0).astype(F32) for o in range(OWNERS)], axis=0
    ).astype(BF16)
    r = lax.broadcasted_iota(I32, (128, 256), 0)
    c = lax.broadcasted_iota(I32, (128, 256), 1)
    tri = jnp.where((r < c) | (c >= 128), 1.0, 0.0).astype(F32).astype(BF16)
    counts = nn(masks, tri)
    prefix = counts[:, :128]
    totals = counts[:, 128:].astype(BF16)
    wide = jnp.concatenate([totals[o * 64 : (o + 1) * 64] for o in range(OWNERS)], axis=1)
    r = lax.broadcasted_iota(I32, (64, 64), 0)
    c = lax.broadcasted_iota(I32, (64, 64), 1)
    low = jnp.where(c < r, 1.0, 0.0).astype(F32).astype(BF16)
    before = nn(low, wide)
    rank = jnp.zeros((64, 128), F32)
    for o in range(OWNERS):
        here = prefix[o * 64 : (o + 1) * 64] + before[:, o * 128 : (o + 1) * 128]
        rank = jnp.where(owner == o, here, rank)

    sub = lax.broadcasted_iota(I32, (8, CH), 0)
    target = iota_bf16((8, 16, CH), lambda g, s, c: (g * 2 + s // 8) * 2 + s % 2)

    score = split3(docs_ref[1])
    weight = split3(docs_ref[2])
    slot = dest & (DOC - 1)
    zero = jnp.zeros((64, 128), F32)
    fields = (
        (score[0], weight[0], (slot & 8128).astype(F32), score[2]),
        (score[1], weight[1], (slot & 63).astype(F32), zero),
    )
    place = owner * 512 + rank.astype(I32)
    pos_ref[...] = place
    for t in range(DOC // CH):
        rows = slice(t * 8, t * 8 + 8)
        cols = slice(t * CH, t * CH + CH)
        pos = lanes(place[rows])
        b_ref[:, cols] = one_hot(pos & 255, 256, CH)
        hit = target == rows16(pos >> 8)[None]
        for p in range(2):
            part = [jnp.broadcast_to(lanes(v[rows]), (8, CH)) for v in fields[p]]
            vals = jnp.where(
                sub < 4,
                jnp.where(sub < 2, part[0], part[1]),
                jnp.where(sub < 6, part[2], part[3]),
            )
            both = jnp.concatenate([vals, vals], axis=0).astype(BF16)
            a_ref[p * 128 : (p + 1) * 128, cols] = jnp.where(
                hit, both[None], jnp.zeros((), BF16)
            ).reshape(128, CH)
    table = nt(a_ref[...], b_ref[...])
    send_ref[...] = (table[0:128] + table[128:256]).reshape(OWNERS, 8, 256)


def route(docs):
    return pl.pallas_call(
        route_body,
        out_shape=(
            jax.ShapeDtypeStruct((OWNERS, 8, 256), F32),
            jax.ShapeDtypeStruct((64, 128), I32),
        ),
        scratch_shapes=[pltpu.VMEM((256, DOC), BF16), pltpu.VMEM((256, DOC), BF16)],
        in_specs=[pl.BlockSpec(memory_space=pltpu.VMEM)],
        out_specs=(pl.BlockSpec(memory_space=pltpu.VMEM), pl.BlockSpec(memory_space=pltpu.VMEM)),
        compiler_params=pltpu.CompilerParams(vmem_limit_bytes=24 << 20),
        cost_estimate=pl.CostEstimate(flops=2000000000, transcendentals=0, bytes_accessed=10000000),
        name="route",
    )(docs)


def owner_body(rec_ref, query_ref, clicks_ref, out_ref, a_ref, b_ref, h_ref):
    it = iota_bf16((2, 16, 512), lambda g, s, c: g * 16 + s)
    for o in range(OWNERS):
        tile = rec_ref[o]
        cols = slice(o * 512, o * 512 + 512)
        pick = lambda n: jnp.concatenate([tile[2 * n : 2 * n + 1], tile[2 * n + 1 : 2 * n + 2]], axis=1)
        slot = pick(2).astype(I32)
        b_ref[:, cols] = one_hot(slot & 255, 256, 512)
        block = slot >> 8
        h_ref[o : o + 1, :] = block
        hit = it == rows16(block)[None]
        s3 = split3(pick(0) + pick(3))
        w3 = split3(pick(1))
        for n, v in enumerate((s3[0], w3[0], s3[1], w3[1], s3[2])):
            a_ref[n * 32 : n * 32 + 32, cols] = jnp.where(
                hit, rows16(v)[None], jnp.zeros((), BF16)
            ).reshape(32, 512)
    table = nt(a_ref[...], b_ref[...])
    score = table[0:32] + table[64:96] + table[128:160]
    weight = table[32:64] + table[96:128]

    def wide(ref):
        return jnp.concatenate([ref[pl.ds(0, 32, stride=2), :], ref[pl.ds(1, 32, stride=2), :]], axis=1)

    query = wide(query_ref)
    clicks = wide(clicks_ref)
    lane = lax.broadcasted_iota(I32, (32, 256), 1)
    steps = [1 << k for k in range(8)]
    fore = [(pltpu.roll(query, d, 1) == query) & (lane >= d) for d in steps]
    back = [(pltpu.roll(query, 256 - d, 1) == query) & (lane < 256 - d) for d in steps]

    def scans(x, op):
        y = x
        for d, f, b in zip(steps, fore, back):
            x = jnp.where(f, op(x, pltpu.roll(x, d, 1)), x)
            y = jnp.where(b, op(y, pltpu.roll(y, 256 - d, 1)), y)
        return x, y

    top = jnp.maximum(*scans(score, jnp.maximum))
    scaled = weight * jnp.exp(score - top)
    gain = weight * clicks.astype(F32)

    def total(x):
        left, right = scans(x, jnp.add)
        return left + (right - x)

    denominator = total(scaled)
    clicked = total(gain)
    chance = scaled / denominator
    gradient = (gain - clicked * chance).astype(BF16)
    curvature = (clicked * chance * (1.0 - chance)).astype(BF16)
    stats = jnp.concatenate([gradient, curvature], axis=0)
    picked = nn(stats, b_ref[...])
    sub = lax.broadcasted_iota(I32, (32, 128), 0)
    for o in range(OWNERS):
        rows = []
        for q in range(4):
            at = o * 512 + q * 128
            hit = sub == h_ref[o : o + 1, q * 128 : (q + 1) * 128]
            for k in range(2):
                part = picked[k * 32 : (k + 1) * 32, at : at + 128]
                rows.append(jnp.sum(jnp.where(hit, part, 0.0), axis=0, keepdims=True))
        out_ref[o] = jnp.concatenate(rows, axis=0)


def owner(rec, query, clicks):
    return pl.pallas_call(
        owner_body,
        out_shape=jax.ShapeDtypeStruct((OWNERS, 8, 128), F32),
        scratch_shapes=[
            pltpu.VMEM((160, DOC), BF16),
            pltpu.VMEM((256, DOC), BF16),
            pltpu.VMEM((OWNERS, 512), I32),
        ],
        in_specs=[pl.BlockSpec(memory_space=pltpu.VMEM)] * 3,
        out_specs=pl.BlockSpec(memory_space=pltpu.VMEM),
        compiler_params=pltpu.CompilerParams(vmem_limit_bytes=24 << 20),
        cost_estimate=pl.CostEstimate(flops=4000000000, transcendentals=0, bytes_accessed=15000000),
        name="owner",
    )(rec, query, clicks)


F8 = jnp.float8_e4m3fn
LOW = 16.0
GF = 8
PB = 8


def one_hot8(row, cols):
    it = (lax.broadcasted_iota(I32, (4, 32, cols), 0) * 32 + lax.broadcasted_iota(I32, (4, 32, cols), 1)).astype(jnp.int8)
    r = jnp.broadcast_to(row, (32, cols)).astype(jnp.int8)
    return jnp.where(it == r[None], jnp.ones((), F8), jnp.zeros((), F8)).reshape(128, cols)


def hist_body(back_ref, pos_ref, leaf_ref, bins_ref, send_ref, spread_ref, down_ref):
    @pl.when(pl.program_id(0) == 0)
    def _():
        back = back_ref[...].reshape(128, 128)
        table = back.astype(BF16)
        sub8 = lax.broadcasted_iota(I32, (8, 128), 0)
        peak = jnp.max(jnp.abs(back_ref[...]), axis=0)
        peak = jnp.max(peak, axis=1, keepdims=True)
        odd = lax.broadcasted_iota(I32, (8, 1), 0) % 2
        top0 = jnp.max(jnp.where(odd == 0, peak, 0.0), axis=0, keepdims=True)
        top1 = jnp.max(jnp.where(odd == 1, peak, 0.0), axis=0, keepdims=True)
        top = jnp.where(odd == 0, top0, top1)
        up = jnp.full((8, 1), 2.0**-20, F32)
        down = jnp.full((8, 1), 2.0**20, F32)
        for e in (64, 32, 16, 8, 4, 2, 1):
            fits = top * (up * 2.0**e) <= 448.0
            up = jnp.where(fits, up * 2.0**e, up)
            down = jnp.where(fits, down * 2.0**-e, down)
        up = jnp.broadcast_to(up, (8, CH))

        for t in range(DOC // CH):
            rows = slice(t * 8, t * 8 + 8)
            pos = lanes(pos_ref[rows, :])
            leaf = lanes(leaf_ref[rows, :])
            picked = nn(table, one_hot(pos & 127, 128, CH))
            hi = jnp.broadcast_to(pos >> 7, (8, CH))
            quarter = lax.broadcasted_iota(I32, (8, CH), 0) // 2
            acc = jnp.zeros((8, CH), F32)
            for o in range(OWNERS):
                acc = acc + jnp.where(hi == quarter + 4 * o, picked[o * 8 : (o + 1) * 8], 0.0)
            acc = acc + pltpu.roll(acc, 4, 0)
            acc = acc + pltpu.roll(acc, 2, 0)
            acc = acc * up
            high = acc.astype(F8).astype(F32)
            low = (acc - high) * LOW
            it = iota_bf16((8, 16, CH), lambda g, s, c: g * 8 + s // 2)
            hit = it == rows16(leaf)[None]
            for n, v in enumerate((high, low)):
                both = jnp.concatenate([v, v], axis=0).astype(BF16)
                spread_ref[n * 128 : (n + 1) * 128, t * CH : t * CH + CH] = (
                    jnp.where(hit, both[None], jnp.zeros((), BF16)).reshape(128, CH).astype(F8)
                )
        down_ref[...] = jnp.broadcast_to(down, (8, 128))

    scale = down_ref[...][None]
    hot = jnp.concatenate([one_hot8(bins_ref[j : j + 1, :], DOC) for j in range(GF)], axis=0)
    acc = nt(spread_ref[...], hot)
    acc = acc[:128] + acc[128:] * (1.0 / LOW)
    cut = [
        (acc[:, 128 * j : 128 * j + 128].reshape(OWNERS, 8, 128) * scale).reshape(OWNERS, 1, 8, 128)
        for j in range(GF)
    ]
    send_ref[...] = (
        jnp.concatenate(cut, axis=1).reshape(OWNERS, GF // 2, 16, 128).astype(BF16)
    )


def hist(back, pos, leaf, bins):
    whole = lambda a: pl.BlockSpec(a.shape, lambda p: (0,) * a.ndim)
    return pl.pallas_call(
        hist_body,
        grid=(F_DEV // GF,),
        in_specs=[whole(back), whole(pos), whole(leaf), pl.BlockSpec((GF, DOC), lambda p: (p, 0))],
        out_specs=pl.BlockSpec((OWNERS, GF // 2, 16, 128), lambda p: (0, p, 0, 0)),
        out_shape=jax.ShapeDtypeStruct((OWNERS, F_DEV // 2, 16, 128), BF16),
        scratch_shapes=[pltpu.VMEM((256, DOC), F8), pltpu.VMEM((8, 128), F32)],
        compiler_params=pltpu.CompilerParams(vmem_limit_bytes=40 << 20),
        cost_estimate=pl.CostEstimate(flops=18000000000, transcendentals=0, bytes_accessed=40000000),
        name="hist",
    )(back, pos, leaf, bins)


def total_body(rec_ref, out_ref):
    for p in range(PB):
        acc = rec_ref[0, p].astype(F32)
        for o in range(1, OWNERS):
            acc = acc + rec_ref[o, p].astype(F32)
        for j in range(2):
            for l in range(4):
                out_ref[l, 4 * p + 2 * j : 4 * p + 2 * j + 2, :] = acc[8 * j + 2 * l : 8 * j + 2 * l + 2]


def total(rec):
    return pl.pallas_call(
        total_body,
        grid=(F_DEV // 2 // PB,),
        in_specs=[pl.BlockSpec((OWNERS, PB, 16, 128), lambda p: (0, p, 0, 0))],
        out_specs=pl.BlockSpec((4, 4 * PB, 128), lambda p: (0, p, 0)),
        out_shape=jax.ShapeDtypeStruct((4, 2 * F_DEV, 128), F32),
        compiler_params=pltpu.CompilerParams(vmem_limit_bytes=16 << 20),
        name="total",
    )(rec)


def shards(feature_bins, leaf_index, doc_scores, doc_weights, destination, query_ids, clicks):
    tall = lambda a: a.reshape(64, 128)
    swap = lambda a: lax.all_to_all(a, "rows", split_axis=0, concat_axis=0, tiled=True)
    send, pos = route(jnp.stack([tall(destination).astype(F32), tall(doc_scores), tall(doc_weights)]))
    back = owner(swap(send), tall(query_ids), tall(clicks))
    parts = hist(swap(back), pos, tall(leaf_index), feature_bins)
    return total(swap(parts)).reshape(4, F_DEV, 2, BINS)


def solution(mesh):
    placed = (P("feat", "rows"), P("rows"), P("rows"), P("rows"), P("rows"), P("rows"), P("rows"))
    return jax.shard_map(
        shards, mesh=mesh, in_specs=placed, out_specs=P("rows", "feat", None, None), check_vma=False
    )
```

```python
import jax
import jax.numpy as jnp
from jax import lax
from jax.experimental import pallas as pl
from jax.experimental.pallas import tpu as pltpu
from jax.sharding import PartitionSpec as P

BINS = 128
LEAVES = 64
QBLOCK = 256
OWNERS = 16
DOC = 8192
F_DEV = 32
CH = 1024
F32 = jnp.float32
BF16 = jnp.bfloat16
I32 = jnp.int32


def nt(a, b):
    return lax.dot_general(a, b, (((1,), (1,)), ((), ())), preferred_element_type=F32)


def nn(a, b):
    return lax.dot_general(a, b, (((1,), (0,)), ((), ())), preferred_element_type=F32)


def lanes(tile):
    return jnp.concatenate([tile[r : r + 1, :] for r in range(tile.shape[0])], axis=1)


def rows16(row):
    return jnp.broadcast_to(row.astype(F32), (16, row.shape[1])).astype(BF16)


def iota_bf16(shape, fn):
    parts = [lax.broadcasted_iota(I32, shape, d) for d in range(len(shape))]
    return fn(*parts).astype(F32).astype(BF16)


def split3(x):
    a = x.astype(BF16).astype(F32)
    r = x - a
    b = r.astype(BF16).astype(F32)
    return a, b, r - b


def one_hot(row, width, cols):
    it = iota_bf16((width // 16, 16, cols), lambda g, s, c: g * 16 + s)
    hit = it == rows16(row)[None]
    one = jnp.ones((), BF16)
    zero = jnp.zeros((), BF16)
    return jnp.where(hit, one, zero).reshape(width, cols)


def route_body(docs_ref, send_ref, pos_ref, a_ref, b_ref):
    dest = docs_ref[0].astype(I32)
    owner = dest >> 13
    masks = jnp.concatenate(
        [jnp.where(owner == o, 1.0, 0.0).astype(F32) for o in range(OWNERS)], axis=0
    ).astype(BF16)
    r = lax.broadcasted_iota(I32, (128, 256), 0)
    c = lax.broadcasted_iota(I32, (128, 256), 1)
    tri = jnp.where((r < c) | (c >= 128), 1.0, 0.0).astype(F32).astype(BF16)
    counts = nn(masks, tri)
    prefix = counts[:, :128]
    totals = counts[:, 128:].astype(BF16)
    wide = jnp.concatenate([totals[o * 64 : (o + 1) * 64] for o in range(OWNERS)], axis=1)
    r = lax.broadcasted_iota(I32, (64, 64), 0)
    c = lax.broadcasted_iota(I32, (64, 64), 1)
    low = jnp.where(c < r, 1.0, 0.0).astype(F32).astype(BF16)
    before = nn(low, wide)
    rank = jnp.zeros((64, 128), F32)
    for o in range(OWNERS):
        here = prefix[o * 64 : (o + 1) * 64] + before[:, o * 128 : (o + 1) * 128]
        rank = jnp.where(owner == o, here, rank)

    sub = lax.broadcasted_iota(I32, (8, CH), 0)
    target = iota_bf16((8, 16, CH), lambda g, s, c: (g * 2 + s // 8) * 2 + s % 2)

    score = split3(docs_ref[1])
    weight = split3(docs_ref[2])
    slot = dest & (DOC - 1)
    zero = jnp.zeros((64, 128), F32)
    fields = (
        (score[0], weight[0], (slot & 8128).astype(F32), score[2]),
        (score[1], weight[1], (slot & 63).astype(F32), zero),
    )
    place = owner * 512 + rank.astype(I32)
    pos_ref[...] = place
    for t in range(DOC // CH):
        rows = slice(t * 8, t * 8 + 8)
        cols = slice(t * CH, t * CH + CH)
        pos = lanes(place[rows])
        b_ref[:, cols] = one_hot(pos & 255, 256, CH)
        hit = target == rows16(pos >> 8)[None]
        for p in range(2):
            part = [jnp.broadcast_to(lanes(v[rows]), (8, CH)) for v in fields[p]]
            vals = jnp.where(
                sub < 4,
                jnp.where(sub < 2, part[0], part[1]),
                jnp.where(sub < 6, part[2], part[3]),
            )
            both = jnp.concatenate([vals, vals], axis=0).astype(BF16)
            a_ref[p * 128 : (p + 1) * 128, cols] = jnp.where(
                hit, both[None], jnp.zeros((), BF16)
            ).reshape(128, CH)
    table = nt(a_ref[...], b_ref[...])
    send_ref[...] = (table[0:128] + table[128:256]).reshape(OWNERS, 8, 256)


def route(docs):
    return pl.pallas_call(
        route_body,
        out_shape=(
            jax.ShapeDtypeStruct((OWNERS, 8, 256), F32),
            jax.ShapeDtypeStruct((64, 128), I32),
        ),
        scratch_shapes=[pltpu.VMEM((256, DOC), BF16), pltpu.VMEM((256, DOC), BF16)],
        in_specs=[pl.BlockSpec(memory_space=pltpu.VMEM)],
        out_specs=(pl.BlockSpec(memory_space=pltpu.VMEM), pl.BlockSpec(memory_space=pltpu.VMEM)),
        compiler_params=pltpu.CompilerParams(vmem_limit_bytes=24 << 20),
        cost_estimate=pl.CostEstimate(flops=2000000000, transcendentals=0, bytes_accessed=10000000),
        name="route",
    )(docs)


def owner_body(rec_ref, query_ref, clicks_ref, out_ref, a_ref, b_ref, h_ref):
    it = iota_bf16((2, 16, 512), lambda g, s, c: g * 16 + s)
    for o in range(OWNERS):
        tile = rec_ref[o]
        cols = slice(o * 512, o * 512 + 512)
        pick = lambda n: jnp.concatenate([tile[2 * n : 2 * n + 1], tile[2 * n + 1 : 2 * n + 2]], axis=1)
        slot = pick(2).astype(I32)
        b_ref[:, cols] = one_hot(slot & 255, 256, 512)
        block = slot >> 8
        h_ref[o : o + 1, :] = block
        hit = it == rows16(block)[None]
        s3 = split3(pick(0) + pick(3))
        w3 = split3(pick(1))
        for n, v in enumerate((s3[0], w3[0], s3[1], w3[1], s3[2])):
            a_ref[n * 32 : n * 32 + 32, cols] = jnp.where(
                hit, rows16(v)[None], jnp.zeros((), BF16)
            ).reshape(32, 512)
    table = nt(a_ref[...], b_ref[...])
    score = table[0:32] + table[64:96] + table[128:160]
    weight = table[32:64] + table[96:128]

    def wide(ref):
        return jnp.concatenate([ref[pl.ds(0, 32, stride=2), :], ref[pl.ds(1, 32, stride=2), :]], axis=1)

    query = wide(query_ref)
    clicks = wide(clicks_ref)
    lane = lax.broadcasted_iota(I32, (32, 256), 1)
    steps = [1 << k for k in range(8)]
    fore = [(pltpu.roll(query, d, 1) == query) & (lane >= d) for d in steps]
    back = [(pltpu.roll(query, 256 - d, 1) == query) & (lane < 256 - d) for d in steps]

    def scans(x, op):
        y = x
        for d, f, b in zip(steps, fore, back):
            x = jnp.where(f, op(x, pltpu.roll(x, d, 1)), x)
            y = jnp.where(b, op(y, pltpu.roll(y, 256 - d, 1)), y)
        return x, y

    top = jnp.maximum(*scans(score, jnp.maximum))
    scaled = weight * jnp.exp(score - top)
    gain = weight * clicks.astype(F32)

    def total(x):
        left, right = scans(x, jnp.add)
        return left + (right - x)

    denominator = total(scaled)
    clicked = total(gain)
    chance = scaled / denominator
    gradient = (gain - clicked * chance).astype(BF16)
    curvature = (clicked * chance * (1.0 - chance)).astype(BF16)
    stats = jnp.concatenate([gradient, curvature], axis=0)
    picked = nn(stats, b_ref[...])
    sub = lax.broadcasted_iota(I32, (32, 128), 0)
    for o in range(OWNERS):
        rows = []
        for q in range(4):
            at = o * 512 + q * 128
            hit = sub == h_ref[o : o + 1, q * 128 : (q + 1) * 128]
            for k in range(2):
                part = picked[k * 32 : (k + 1) * 32, at : at + 128]
                rows.append(jnp.sum(jnp.where(hit, part, 0.0), axis=0, keepdims=True))
        out_ref[o] = jnp.concatenate(rows, axis=0)


def owner(rec, query, clicks):
    return pl.pallas_call(
        owner_body,
        out_shape=jax.ShapeDtypeStruct((OWNERS, 8, 128), F32),
        scratch_shapes=[
            pltpu.VMEM((160, DOC), BF16),
            pltpu.VMEM((256, DOC), BF16),
            pltpu.VMEM((OWNERS, 512), I32),
        ],
        in_specs=[pl.BlockSpec(memory_space=pltpu.VMEM)] * 3,
        out_specs=pl.BlockSpec(memory_space=pltpu.VMEM),
        compiler_params=pltpu.CompilerParams(vmem_limit_bytes=24 << 20),
        cost_estimate=pl.CostEstimate(flops=4000000000, transcendentals=0, bytes_accessed=15000000),
        name="owner",
    )(rec, query, clicks)


F8 = jnp.float8_e4m3fn
LOW = 16.0
GF = 8
PB = 8


def one_hot8(row, cols):
    it = (lax.broadcasted_iota(I32, (4, 32, cols), 0) * 32 + lax.broadcasted_iota(I32, (4, 32, cols), 1)).astype(jnp.int8)
    r = jnp.broadcast_to(row, (32, cols)).astype(jnp.int8)
    return jnp.where(it == r[None], jnp.ones((), F8), jnp.zeros((), F8)).reshape(128, cols)


def hist_body(back_ref, pos_ref, leaf_ref, bins_ref, send_ref, spread_ref):
    back = back_ref[...].reshape(128, 128)
    table = back.astype(BF16)
    sub8 = lax.broadcasted_iota(I32, (8, 128), 0)
    peak = jnp.max(jnp.abs(back_ref[...]), axis=0)
    peak = jnp.max(peak, axis=1, keepdims=True)
    odd = lax.broadcasted_iota(I32, (8, 1), 0) % 2
    top0 = jnp.max(jnp.where(odd == 0, peak, 0.0), axis=0, keepdims=True)
    top1 = jnp.max(jnp.where(odd == 1, peak, 0.0), axis=0, keepdims=True)
    top = jnp.where(odd == 0, top0, top1)
    up = jnp.full((8, 1), 2.0**-20, F32)
    down = jnp.full((8, 1), 2.0**20, F32)
    for e in (64, 32, 16, 8, 4, 2, 1):
        fits = top * (up * 2.0**e) <= 448.0
        up = jnp.where(fits, up * 2.0**e, up)
        down = jnp.where(fits, down * 2.0**-e, down)
    up = jnp.broadcast_to(up, (8, CH))

    for t in range(DOC // CH):
        rows = slice(t * 8, t * 8 + 8)
        pos = lanes(pos_ref[rows, :])
        leaf = lanes(leaf_ref[rows, :])
        picked = nn(table, one_hot(pos & 127, 128, CH))
        hi = jnp.broadcast_to(pos >> 7, (8, CH))
        quarter = lax.broadcasted_iota(I32, (8, CH), 0) // 2
        acc = jnp.zeros((8, CH), F32)
        for o in range(OWNERS):
            acc = acc + jnp.where(hi == quarter + 4 * o, picked[o * 8 : (o + 1) * 8], 0.0)
        acc = acc + pltpu.roll(acc, 4, 0)
        acc = acc + pltpu.roll(acc, 2, 0)
        acc = acc * up
        high = acc.astype(F8).astype(F32)
        low = (acc - high) * LOW
        it = iota_bf16((8, 16, CH), lambda g, s, c: g * 8 + s // 2)
        hit = it == rows16(leaf)[None]
        for n, v in enumerate((high, low)):
            both = jnp.concatenate([v, v], axis=0).astype(BF16)
            spread_ref[n * 128 : (n + 1) * 128, t * CH : t * CH + CH] = (
                jnp.where(hit, both[None], jnp.zeros((), BF16)).reshape(128, CH).astype(F8)
            )
    scale = jnp.broadcast_to(down, (8, 128))[None]

    def group(p, carry):
        tile = bins_ref[pl.ds(p * GF, GF), :]
        hot = jnp.concatenate([one_hot8(tile[j : j + 1, :], DOC) for j in range(GF)], axis=0)
        acc = nt(spread_ref[...], hot)
        acc = acc[:128] + acc[128:] * (1.0 / LOW)
        cut = [
            (acc[:, 128 * j : 128 * j + 128].reshape(OWNERS, 8, 128) * scale).reshape(OWNERS, 1, 8, 128)
            for j in range(GF)
        ]
        send_ref[:, pl.ds(p * (GF // 2), GF // 2)] = (
            jnp.concatenate(cut, axis=1).reshape(OWNERS, GF // 2, 16, 128).astype(BF16)
        )
        return carry

    for p in range(F_DEV // GF):
        group(p, 0)


def hist(back, pos, leaf, bins):
    vmem = pl.BlockSpec(memory_space=pltpu.VMEM)
    return pl.pallas_call(
        hist_body,
        in_specs=[vmem] * 4,
        out_specs=vmem,
        out_shape=jax.ShapeDtypeStruct((OWNERS, F_DEV // 2, 16, 128), BF16),
        scratch_shapes=[pltpu.VMEM((256, DOC), F8)],
        compiler_params=pltpu.CompilerParams(vmem_limit_bytes=40 << 20),
        cost_estimate=pl.CostEstimate(flops=18000000000, transcendentals=0, bytes_accessed=40000000),
        name="hist",
    )(back, pos, leaf, bins)


def total_body(rec_ref, out_ref):
    for p in range(PB):
        acc = rec_ref[0, p].astype(F32)
        for o in range(1, OWNERS):
            acc = acc + rec_ref[o, p].astype(F32)
        for j in range(2):
            for l in range(4):
                out_ref[l, 4 * p + 2 * j : 4 * p + 2 * j + 2, :] = acc[8 * j + 2 * l : 8 * j + 2 * l + 2]


def total(rec):
    return pl.pallas_call(
        total_body,
        grid=(F_DEV // 2 // PB,),
        in_specs=[pl.BlockSpec((OWNERS, PB, 16, 128), lambda p: (0, p, 0, 0))],
        out_specs=pl.BlockSpec((4, 4 * PB, 128), lambda p: (0, p, 0)),
        out_shape=jax.ShapeDtypeStruct((4, 2 * F_DEV, 128), F32),
        compiler_params=pltpu.CompilerParams(vmem_limit_bytes=16 << 20),
        name="total",
    )(rec)


def shards(feature_bins, leaf_index, doc_scores, doc_weights, destination, query_ids, clicks):
    tall = lambda a: a.reshape(64, 128)
    swap = lambda a: lax.all_to_all(a, "rows", split_axis=0, concat_axis=0, tiled=True)
    send, pos = route(jnp.stack([tall(destination).astype(F32), tall(doc_scores), tall(doc_weights)]))
    back = owner(swap(send), tall(query_ids), tall(clicks))
    parts = hist(swap(back), pos, tall(leaf_index), feature_bins)
    return total(swap(parts)).reshape(4, F_DEV, 2, BINS)


def solution(mesh):
    placed = (P("feat", "rows"), P("rows"), P("rows"), P("rows"), P("rows"), P("rows"), P("rows"))
    return jax.shard_map(
        shards, mesh=mesh, in_specs=placed, out_specs=P("rows", "feat", None, None), check_vma=False
    )
```

```python
import jax
import jax.numpy as jnp
from jax import lax
from jax.experimental import pallas as pl
from jax.experimental.pallas import tpu as pltpu
from jax.sharding import PartitionSpec as P

BINS = 128
LEAVES = 64
QBLOCK = 256
OWNERS = 16
DOC = 8192
F_DEV = 32
CH = 1024
F32 = jnp.float32
BF16 = jnp.bfloat16
I32 = jnp.int32


def nt(a, b):
    return lax.dot_general(a, b, (((1,), (1,)), ((), ())), preferred_element_type=F32)


def nn(a, b):
    return lax.dot_general(a, b, (((1,), (0,)), ((), ())), preferred_element_type=F32)


def lanes(tile):
    return jnp.concatenate([tile[r : r + 1, :] for r in range(tile.shape[0])], axis=1)


def rows16(row):
    return jnp.broadcast_to(row.astype(F32), (16, row.shape[1])).astype(BF16)


def iota_bf16(shape, fn):
    parts = [lax.broadcasted_iota(I32, shape, d) for d in range(len(shape))]
    return fn(*parts).astype(F32).astype(BF16)


def split3(x):
    a = x.astype(BF16).astype(F32)
    r = x - a
    b = r.astype(BF16).astype(F32)
    return a, b, r - b


def one_hot(row, width, cols):
    it = iota_bf16((width // 16, 16, cols), lambda g, s, c: g * 16 + s)
    hit = it == rows16(row)[None]
    one = jnp.ones((), BF16)
    zero = jnp.zeros((), BF16)
    return jnp.where(hit, one, zero).reshape(width, cols)


def route_body(docs_ref, send_ref, pos_ref, a_ref, b_ref):
    dest = docs_ref[0].astype(I32)
    owner = dest >> 13
    masks = jnp.concatenate(
        [jnp.where(owner == o, 1.0, 0.0).astype(F32) for o in range(OWNERS)], axis=0
    ).astype(BF16)
    r = lax.broadcasted_iota(I32, (128, 256), 0)
    c = lax.broadcasted_iota(I32, (128, 256), 1)
    tri = jnp.where((r < c) | (c >= 128), 1.0, 0.0).astype(F32).astype(BF16)
    counts = nn(masks, tri)
    prefix = counts[:, :128]
    totals = counts[:, 128:].astype(BF16)
    wide = jnp.concatenate([totals[o * 64 : (o + 1) * 64] for o in range(OWNERS)], axis=1)
    r = lax.broadcasted_iota(I32, (64, 64), 0)
    c = lax.broadcasted_iota(I32, (64, 64), 1)
    low = jnp.where(c < r, 1.0, 0.0).astype(F32).astype(BF16)
    before = nn(low, wide)
    rank = jnp.zeros((64, 128), F32)
    for o in range(OWNERS):
        here = prefix[o * 64 : (o + 1) * 64] + before[:, o * 128 : (o + 1) * 128]
        rank = jnp.where(owner == o, here, rank)

    sub = lax.broadcasted_iota(I32, (8, CH), 0)
    target = iota_bf16((8, 16, CH), lambda g, s, c: (g * 2 + s // 8) * 2 + s % 2)

    score = split3(docs_ref[1])
    weight = split3(docs_ref[2])
    slot = dest & (DOC - 1)
    zero = jnp.zeros((64, 128), F32)
    fields = (
        (score[0], weight[0], (slot & 8128).astype(F32), score[2]),
        (score[1], weight[1], (slot & 63).astype(F32), zero),
    )
    place = owner * 512 + rank.astype(I32)
    pos_ref[...] = place
    for t in range(DOC // CH):
        rows = slice(t * 8, t * 8 + 8)
        cols = slice(t * CH, t * CH + CH)
        pos = lanes(place[rows])
        b_ref[:, cols] = one_hot(pos & 255, 256, CH)
        hit = target == rows16(pos >> 8)[None]
        for p in range(2):
            part = [jnp.broadcast_to(lanes(v[rows]), (8, CH)) for v in fields[p]]
            vals = jnp.where(
                sub < 4,
                jnp.where(sub < 2, part[0], part[1]),
                jnp.where(sub < 6, part[2], part[3]),
            )
            both = jnp.concatenate([vals, vals], axis=0).astype(BF16)
            a_ref[p * 128 : (p + 1) * 128, cols] = jnp.where(
                hit, both[None], jnp.zeros((), BF16)
            ).reshape(128, CH)
    table = nt(a_ref[...], b_ref[...])
    send_ref[...] = (table[0:128] + table[128:256]).reshape(OWNERS, 8, 256)


def route(docs):
    return pl.pallas_call(
        route_body,
        out_shape=(
            jax.ShapeDtypeStruct((OWNERS, 8, 256), F32),
            jax.ShapeDtypeStruct((64, 128), I32),
        ),
        scratch_shapes=[pltpu.VMEM((256, DOC), BF16), pltpu.VMEM((256, DOC), BF16)],
        in_specs=[pl.BlockSpec(memory_space=pltpu.VMEM)],
        out_specs=(pl.BlockSpec(memory_space=pltpu.VMEM), pl.BlockSpec(memory_space=pltpu.VMEM)),
        compiler_params=pltpu.CompilerParams(vmem_limit_bytes=24 << 20),
        cost_estimate=pl.CostEstimate(flops=2000000000, transcendentals=0, bytes_accessed=10000000),
        name="route",
    )(docs)


def owner_body(rec_ref, query_ref, clicks_ref, out_ref, a_ref, b_ref, h_ref):
    it = iota_bf16((2, 16, 512), lambda g, s, c: g * 16 + s)
    for o in range(OWNERS):
        tile = rec_ref[o]
        cols = slice(o * 512, o * 512 + 512)
        pick = lambda n: jnp.concatenate([tile[2 * n : 2 * n + 1], tile[2 * n + 1 : 2 * n + 2]], axis=1)
        slot = pick(2).astype(I32)
        b_ref[:, cols] = one_hot(slot & 255, 256, 512)
        block = slot >> 8
        h_ref[o : o + 1, :] = block
        hit = it == rows16(block)[None]
        s3 = split3(pick(0) + pick(3))
        w3 = split3(pick(1))
        for n, v in enumerate((s3[0], w3[0], s3[1], w3[1], s3[2])):
            a_ref[n * 32 : n * 32 + 32, cols] = jnp.where(
                hit, rows16(v)[None], jnp.zeros((), BF16)
            ).reshape(32, 512)
    table = nt(a_ref[...], b_ref[...])
    score = table[0:32] + table[64:96] + table[128:160]
    weight = table[32:64] + table[96:128]

    def wide(ref):
        return jnp.concatenate([ref[pl.ds(0, 32, stride=2), :], ref[pl.ds(1, 32, stride=2), :]], axis=1)

    query = wide(query_ref)
    clicks = wide(clicks_ref)
    lane = lax.broadcasted_iota(I32, (32, 256), 1)
    steps = [1 << k for k in range(8)]
    fore = [(pltpu.roll(query, d, 1) == query) & (lane >= d) for d in steps]
    back = [(pltpu.roll(query, 256 - d, 1) == query) & (lane < 256 - d) for d in steps]

    def scans(x, op):
        y = x
        for d, f, b in zip(steps, fore, back):
            x = jnp.where(f, op(x, pltpu.roll(x, d, 1)), x)
            y = jnp.where(b, op(y, pltpu.roll(y, 256 - d, 1)), y)
        return x, y

    top = jnp.maximum(*scans(score, jnp.maximum))
    scaled = weight * jnp.exp(score - top)
    gain = weight * clicks.astype(F32)

    def total(x):
        left, right = scans(x, jnp.add)
        return left + (right - x)

    denominator = total(scaled)
    clicked = total(gain)
    chance = scaled / denominator
    gradient = (gain - clicked * chance).astype(BF16)
    curvature = (clicked * chance * (1.0 - chance)).astype(BF16)
    stats = jnp.concatenate([gradient, curvature], axis=0)
    picked = nn(stats, b_ref[...])
    sub = lax.broadcasted_iota(I32, (32, 128), 0)
    for o in range(OWNERS):
        rows = []
        for q in range(4):
            at = o * 512 + q * 128
            hit = sub == h_ref[o : o + 1, q * 128 : (q + 1) * 128]
            for k in range(2):
                part = picked[k * 32 : (k + 1) * 32, at : at + 128]
                rows.append(jnp.sum(jnp.where(hit, part, 0.0), axis=0, keepdims=True))
        out_ref[o] = jnp.concatenate(rows, axis=0)


def owner(rec, query, clicks):
    return pl.pallas_call(
        owner_body,
        out_shape=jax.ShapeDtypeStruct((OWNERS, 8, 128), F32),
        scratch_shapes=[
            pltpu.VMEM((160, DOC), BF16),
            pltpu.VMEM((256, DOC), BF16),
            pltpu.VMEM((OWNERS, 512), I32),
        ],
        in_specs=[pl.BlockSpec(memory_space=pltpu.VMEM)] * 3,
        out_specs=pl.BlockSpec(memory_space=pltpu.VMEM),
        compiler_params=pltpu.CompilerParams(vmem_limit_bytes=24 << 20),
        cost_estimate=pl.CostEstimate(flops=4000000000, transcendentals=0, bytes_accessed=15000000),
        name="owner",
    )(rec, query, clicks)


F8 = jnp.float8_e4m3fn
LOW = 16.0
GF = 16
PB = 8


def one_hot8(row, cols):
    it = (lax.broadcasted_iota(I32, (4, 32, cols), 0) * 32 + lax.broadcasted_iota(I32, (4, 32, cols), 1)).astype(jnp.int8)
    r = jnp.broadcast_to(row, (32, cols)).astype(jnp.int8)
    return jnp.where(it == r[None], jnp.ones((), F8), jnp.zeros((), F8)).reshape(128, cols)


def hist_body(back_ref, pos_ref, leaf_ref, bins_ref, send_ref, spread_ref):
    back = back_ref[...].reshape(128, 128)
    table = back.astype(BF16)
    sub8 = lax.broadcasted_iota(I32, (8, 128), 0)
    peak = jnp.max(jnp.abs(back_ref[...]), axis=0)
    peak = jnp.max(peak, axis=1, keepdims=True)
    odd = lax.broadcasted_iota(I32, (8, 1), 0) % 2
    top0 = jnp.max(jnp.where(odd == 0, peak, 0.0), axis=0, keepdims=True)
    top1 = jnp.max(jnp.where(odd == 1, peak, 0.0), axis=0, keepdims=True)
    top = jnp.where(odd == 0, top0, top1)
    up = jnp.full((8, 1), 2.0**-20, F32)
    down = jnp.full((8, 1), 2.0**20, F32)
    for e in (64, 32, 16, 8, 4, 2, 1):
        fits = top * (up * 2.0**e) <= 448.0
        up = jnp.where(fits, up * 2.0**e, up)
        down = jnp.where(fits, down * 2.0**-e, down)
    up = jnp.broadcast_to(up, (8, CH))

    for t in range(DOC // CH):
        rows = slice(t * 8, t * 8 + 8)
        pos = lanes(pos_ref[rows, :])
        leaf = lanes(leaf_ref[rows, :])
        picked = nn(table, one_hot(pos & 127, 128, CH))
        hi = jnp.broadcast_to(pos >> 7, (8, CH))
        quarter = lax.broadcasted_iota(I32, (8, CH), 0) // 2
        acc = jnp.zeros((8, CH), F32)
        for o in range(OWNERS):
            acc = acc + jnp.where(hi == quarter + 4 * o, picked[o * 8 : (o + 1) * 8], 0.0)
        acc = acc + pltpu.roll(acc, 4, 0)
        acc = acc + pltpu.roll(acc, 2, 0)
        acc = acc * up
        high = acc.astype(F8).astype(F32)
        low = (acc - high) * LOW
        it = iota_bf16((8, 16, CH), lambda g, s, c: g * 8 + s // 2)
        hit = it == rows16(leaf)[None]
        for n, v in enumerate((high, low)):
            both = jnp.concatenate([v, v], axis=0).astype(BF16)
            spread_ref[n * 128 : (n + 1) * 128, t * CH : t * CH + CH] = (
                jnp.where(hit, both[None], jnp.zeros((), BF16)).reshape(128, CH).astype(F8)
            )
    scale = jnp.broadcast_to(down, (8, 128))[None]

    def group(p, carry):
        tile = bins_ref[pl.ds(p * GF, GF), :]
        hot = jnp.concatenate([one_hot8(tile[j : j + 1, :], DOC) for j in range(GF)], axis=0)
        acc = nt(spread_ref[...], hot)
        acc = acc[:128] + acc[128:] * (1.0 / LOW)
        cut = [
            (acc[:, 128 * j : 128 * j + 128].reshape(OWNERS, 8, 128) * scale).reshape(OWNERS, 1, 8, 128)
            for j in range(GF)
        ]
        send_ref[:, pl.ds(p * (GF // 2), GF // 2)] = (
            jnp.concatenate(cut, axis=1).reshape(OWNERS, GF // 2, 16, 128).astype(BF16)
        )
        return carry

    for p in range(F_DEV // GF):
        group(p, 0)


def hist(back, pos, leaf, bins):
    vmem = pl.BlockSpec(memory_space=pltpu.VMEM)
    return pl.pallas_call(
        hist_body,
        in_specs=[vmem] * 4,
        out_specs=vmem,
        out_shape=jax.ShapeDtypeStruct((OWNERS, F_DEV // 2, 16, 128), BF16),
        scratch_shapes=[pltpu.VMEM((256, DOC), F8)],
        compiler_params=pltpu.CompilerParams(vmem_limit_bytes=40 << 20),
        cost_estimate=pl.CostEstimate(flops=18000000000, transcendentals=0, bytes_accessed=40000000),
        name="hist",
    )(back, pos, leaf, bins)


def total_body(rec_ref, out_ref):
    for p in range(PB):
        acc = rec_ref[0, p].astype(F32)
        for o in range(1, OWNERS):
            acc = acc + rec_ref[o, p].astype(F32)
        for j in range(2):
            for l in range(4):
                out_ref[l, 4 * p + 2 * j : 4 * p + 2 * j + 2, :] = acc[8 * j + 2 * l : 8 * j + 2 * l + 2]


def total(rec):
    return pl.pallas_call(
        total_body,
        grid=(F_DEV // 2 // PB,),
        in_specs=[pl.BlockSpec((OWNERS, PB, 16, 128), lambda p: (0, p, 0, 0))],
        out_specs=pl.BlockSpec((4, 4 * PB, 128), lambda p: (0, p, 0)),
        out_shape=jax.ShapeDtypeStruct((4, 2 * F_DEV, 128), F32),
        compiler_params=pltpu.CompilerParams(vmem_limit_bytes=16 << 20),
        name="total",
    )(rec)


def shards(feature_bins, leaf_index, doc_scores, doc_weights, destination, query_ids, clicks):
    tall = lambda a: a.reshape(64, 128)
    swap = lambda a: lax.all_to_all(a, "rows", split_axis=0, concat_axis=0, tiled=True)
    send, pos = route(jnp.stack([tall(destination).astype(F32), tall(doc_scores), tall(doc_weights)]))
    back = owner(swap(send), tall(query_ids), tall(clicks))
    parts = hist(swap(back), pos, tall(leaf_index), feature_bins)
    return total(swap(parts)).reshape(4, F_DEV, 2, BINS)


def solution(mesh):
    placed = (P("feat", "rows"), P("rows"), P("rows"), P("rows"), P("rows"), P("rows"), P("rows"))
    return jax.shard_map(
        shards, mesh=mesh, in_specs=placed, out_specs=P("rows", "feat", None, None), check_vma=False
    )
```
